32 devices in a mesh: groups: 2 (over y), trades: 8 (over z, x), dates: 2 (over core).
Axes of the slice: x: 2, y: 2, z: 4, core: 2. Of those that a mesh axis runs over, the one named last changes fastest.
Arguments:
- basis_values: bfloat16 [8, 256, 256], P('dates', 'groups'), parts along dimension 1, may hold values from -6 to 6
- coefficients: bfloat16 [8192, 256], P('trades'), may hold values from -0.0625 to 0.0625
- set_map: int32 [8192], P('trades'), may hold values from 0 to 255, as said below
- trade_type: int32 [8192], P('trades'), may hold values from 0 to 15
- type_gain: float32 [8, 16], P('dates'), may hold values from 0.25 to 4
- set_lags: int32 [256], replicated, may hold values from 1 to 2
- thresholds: float32 [256], replicated, may hold values from -1 to 1
Outputs:
- coef_grad: float32 [16384, 256], P(('groups', 'trades'), 'dates'), parts along dimension 0
The draws below stay inside these ranges and needn't reach their ends.
There are 2 independent parts, one for each index of `groups`. The reference program is written for one: setup_inputs(seed, part) draws one part's arguments, and reference() takes and returns one part's arrays. A program takes and returns all parts, laid end to end along the dimension named above; an argument that names none is the same for every part. Nothing has to cross between parts.
Inputs may be any that keep to these rules, and one draw needn't show every extreme that they name: `set_map`: in every aligned block of 1024 trades, exactly 128 trades fall in each group of 32 consecutive netting sets (sets g * 32 to (g + 1) * 32 - 1).
All inputs are finite; a program needn't handle non-finite values.
Results may differ from the reference program's by a relative error of at most 0.0018.
Values may be sent and summed in bfloat16 or wider, within the bound.
A program may use at most 64 MiB of HBM per device.

```python
import math
import jax
import jax.numpy as jnp
from jax import lax

K = 256
NSETS = 256
NTYPE = 16
LAG_MAX = 2
TR_DEV = 1024
TRADES = 8192
PATHS = 128
DATES = 8


def draw_set_map(key, part):
    block_count = TRADES // TR_DEV
    per_group = TR_DEV // block_count
    group_sets = NSETS // block_count
    first_key = jax.random.fold_in(key, 11)
    second_key = jax.random.fold_in(key, 23)
    groups_base = jnp.tile(jnp.arange(block_count, dtype=jnp.int32), per_group)
    block_keys = jax.random.split(first_key, block_count)
    shuffled = jax.vmap(lambda one_key: jax.random.permutation(one_key, groups_base))(block_keys)
    within = jax.random.randint(second_key, (TRADES,), 0, group_sets, dtype=jnp.int32)
    return (shuffled.reshape(TRADES) * group_sets + within).astype(jnp.int32)


def place_ends(drawn, rng, least, high):
    index_at = [jax.random.randint(jax.random.fold_in(rng, axis), (), 0, length) for axis, length in enumerate(drawn.shape)]
    longest = drawn.shape.index(max(drawn.shape))
    next_to = index_at[:longest] + [(index_at[longest] + 1) % drawn.shape[longest]] + index_at[longest + 1:]
    return drawn.at[tuple(index_at)].set(least).at[tuple(next_to)].set(high)


def levels(rng, extent, cuts, low, high):
    factor_of, own = 1.0, jax.random.fold_in(rng, 6)
    for axis_at, blocks in cuts:
        steps = jnp.exp(jax.random.uniform(jax.random.fold_in(own, axis_at), (blocks,), jnp.float32, low / len(cuts), high / len(cuts)))
        factor_of = factor_of * jnp.repeat(steps, extent[axis_at] // blocks).reshape([-1 if axis == axis_at else 1 for axis in range(len(extent))])
    return factor_of


def normal_values(stream_key, shape, deviation, most, cuts=(), kind=jnp.bfloat16):
    result = jax.random.normal(stream_key, shape, jnp.float32) * deviation
    if len(cuts) > 0:
        result = levels(stream_key, shape, cuts, -0.22, 0.18) * result
    return jnp.clip(result, min=-most, max=most).astype(kind)


def setup_inputs(seed: int = 0, part: int = 0) -> dict:
    key_of = jax.random.split(jax.random.key(seed), 8)
    own_keys = jax.random.split(jax.random.fold_in(key_of[7], part), 8)
    return {
        "basis_values": normal_values(own_keys[0], (DATES, PATHS, K), 1.0, 6.0, ((0, 2),)),
        "coefficients": normal_values(key_of[1], (TRADES, K), (K * TRADES // NSETS) ** -0.5, 0.0625, ((0, 8),)),
        "set_map": draw_set_map(jax.random.fold_in(key_of[7], 71), part),
        "trade_type": place_ends(jax.random.randint(key_of[3], (TRADES,), 0, NTYPE), jax.random.fold_in(key_of[3], 1), 0, NTYPE - 1).astype(jnp.int32),
        "type_gain": jnp.clip(jnp.exp(math.log(4.0) - 2.7725887 * jax.random.uniform(key_of[4], (DATES, NTYPE), jnp.float32) ** levels(key_of[4], (DATES, NTYPE), ((0, 2),), -0.2, 0.2)), 0.25, 4.0),
        "set_lags": place_ends(jax.random.randint(key_of[5], (NSETS,), 1, LAG_MAX + 1), jax.random.fold_in(key_of[5], 1), 1, LAG_MAX).astype(jnp.int32),
        "thresholds": jnp.clip(jax.random.uniform(key_of[6], (NSETS,), jnp.float32, -1.0, 1.0), -1.0, 1.0),
    }


def reference(basis_values, coefficients, set_map, trade_type, type_gain, set_lags, thresholds):
    trade_count = coefficients.shape[0]
    block_count = trade_count // TR_DEV
    date_count = basis_values.shape[0]
    path_count = basis_values.shape[1]
    set_ids = jnp.arange(NSETS, dtype=jnp.int32)
    basis_wide = basis_values.astype(jnp.float32)

    def block_inputs(block_index):
        first_row = (block_index * TR_DEV).astype(jnp.int32)
        coef_block = lax.dynamic_slice_in_dim(coefficients, first_row, TR_DEV, 0).astype(jnp.float32)
        set_block = lax.dynamic_slice_in_dim(set_map, first_row, TR_DEV, 0)
        type_block = lax.dynamic_slice_in_dim(trade_type, first_row, TR_DEV, 0)
        trade_gain = jnp.take(type_gain, type_block, axis=1)
        return (coef_block, set_block, trade_gain)

    def add_block(block_index, netted):
        coef_block, set_block, trade_gain = block_inputs(block_index)
        raw_value = jnp.einsum('dpk,tk->dpt', basis_wide, coef_block)
        prices = (raw_value * trade_gain[:, None, :]).astype(jnp.bfloat16)
        prices = lax.optimization_barrier(prices)
        membership = (set_block[:, None] == set_ids[None, :]).astype(jnp.float32)
        return netted + jnp.einsum('dpt,ts->pds', prices.astype(jnp.float32), membership)
    netted = lax.fori_loop(0, block_count, add_block, jnp.zeros((path_count, date_count, NSETS), jnp.float32))
    padded = jnp.pad(netted, ((0, 0), (LAG_MAX, 0), (0, 0)))
    padded_back_zeros = jnp.zeros((path_count, LAG_MAX, NSETS), jnp.float32)
    collateral = jnp.zeros_like(netted)
    for lag_value in range(1, LAG_MAX + 1):
        lag_mask = (set_lags == lag_value).astype(jnp.float32)
        collateral = collateral + lag_mask * padded[:, LAG_MAX - lag_value:LAG_MAX - lag_value + date_count, :]
    exposure = jnp.maximum(netted - collateral - thresholds, 0.0)
    direct_term = exposure * (2.0 / math.sqrt(date_count * path_count))
    padded_back = jnp.concatenate([direct_term, padded_back_zeros], axis=1)
    adjoint = direct_term
    for lag_value in range(1, LAG_MAX + 1):
        lag_mask = (set_lags == lag_value).astype(jnp.float32)
        adjoint = adjoint - lag_mask * padded_back[:, lag_value:lag_value + date_count, :]
    adjoint = lax.optimization_barrier(adjoint.astype(jnp.bfloat16))
    adjoint_wide = adjoint.astype(jnp.float32)

    def grad_block(block_index):
        coef_block, set_block, trade_gain = block_inputs(block_index)
        spread = jnp.take(adjoint_wide, set_block, axis=2)
        scaled = (jnp.transpose(spread, (1, 0, 2)) * trade_gain[:, None, :]).astype(jnp.bfloat16)
        scaled = lax.optimization_barrier(scaled)
        return jnp.einsum('dpt,dpk->tk', scaled.astype(jnp.float32), basis_wide)
    grads = lax.map(grad_block, jnp.arange(block_count, dtype=jnp.int32))
    return grads.reshape(trade_count, K)
```

```python
import functools
import math

import jax
import jax.numpy as jnp
from jax import lax
from jax.experimental import pallas as pl
from jax.experimental.pallas import tpu as pltpu
from jax.sharding import PartitionSpec as P

LAG_MAX = 2
GROUP = 8
CODE_MAX = 32767.0
NT = (((1,), (1,)), ((), ()))


def kernel(
    trade_peers, date_peers, loss_scale,
    gain_ref, basis_ref, coef_ref, set_ref, type_ref, lag_ref, limit_ref,
    out_ref,
    code_send, code_recv, unit_send, unit_recv, adj_send, adj_recv,
    member_ref, gain_cols, basis_rows, scaled_ref, half_send, half_recv,
    code_ss, code_rs, unit_ss, unit_rs, adj_ss, adj_rs, half_ss, half_rs,
):
    peers = trade_peers * date_peers
    my_trade = lax.axis_index("trades")
    my_date = lax.axis_index("dates")
    me = my_trade * date_peers + my_date
    local_dates, path_count, basis_count = basis_ref.shape
    trade_count = coef_ref.shape[0]
    set_count = limit_ref.shape[1]
    type_count = gain_ref.shape[1]
    own_paths = path_count // peers
    groups = peers // GROUP
    group_paths = GROUP * own_paths
    group_rows = local_dates * group_paths
    chunk_rows = local_dates * own_paths
    half = basis_count // date_peers

    def device(index):
        return {"trades": index // date_peers, "dates": index % date_peers}

    barrier = pltpu.get_barrier_semaphore()

    def greet(step, carry):
        pl.semaphore_signal(
            barrier, inc=1, device_id=device(lax.rem(me + step, peers)),
            device_id_type=pl.DeviceIdType.MESH,
        )
        return carry

    lax.fori_loop(1, peers, greet, 0)

    def code_copy(index, slot_here, slot_there):
        return pltpu.make_async_remote_copy(
            src_ref=code_send.at[slot_here], dst_ref=code_recv.at[slot_there],
            send_sem=code_ss.at[slot_here], recv_sem=code_rs.at[slot_there],
            device_id=device(index), device_id_type=pl.DeviceIdType.MESH,
        )

    def unit_copy(index, slot_here, slot_there):
        return pltpu.make_async_remote_copy(
            src_ref=unit_send.at[slot_here], dst_ref=unit_recv.at[slot_there],
            send_sem=unit_ss.at[slot_here], recv_sem=unit_rs.at[slot_there],
            device_id=device(index), device_id_type=pl.DeviceIdType.MESH,
        )

    def adj_copy(index, slot_there):
        return pltpu.make_async_remote_copy(
            src_ref=adj_send.at[index % date_peers], dst_ref=adj_recv.at[slot_there],
            send_sem=adj_ss.at[index], recv_sem=adj_rs.at[slot_there],
            device_id=device(index), device_id_type=pl.DeviceIdType.MESH,
        )

    types = type_ref[...]
    gains = []
    for d in range(local_dates):
        row = jnp.zeros_like(types, dtype=jnp.float32)
        for y in range(type_count):
            row = jnp.where(types == y, gain_ref[d, y], row)
        gains.append(row)
    set_ids = lax.broadcasted_iota(jnp.int32, (set_count, trade_count), 0)
    member_wide = jnp.where(set_ids == set_ref[...], 1.0, 0.0)
    member = member_wide.astype(jnp.bfloat16)

    my_group = me // GROUP

    def forward(step, carry):
        group = lax.rem(my_group + 1 + step, groups)
        rows = basis_ref[:, pl.ds(pl.multiple_of(group * group_paths, group_paths), group_paths), :]
        raw = lax.dot_general(
            rows.reshape(group_rows, basis_count), coef_ref[...], NT,
            preferred_element_type=jnp.float32,
        )
        prices = jnp.concatenate(
            [raw[d * group_paths:(d + 1) * group_paths] * gains[d] for d in range(local_dates)], axis=0
        ).astype(jnp.bfloat16)
        part = lax.dot_general(prices, member, NT, preferred_element_type=jnp.float32)
        part = part.reshape(local_dates, GROUP, own_paths, set_count)
        for i in range(GROUP):
            chunk = part[:, i].reshape(chunk_rows, set_count)
            top = jnp.maximum(jnp.max(jnp.abs(chunk), axis=0, keepdims=True), 1e-30)
            codes = jnp.round(chunk * (CODE_MAX / top)).astype(jnp.int32)
            code_send[group * GROUP + i] = codes.astype(jnp.int16)
            unit_send[group * GROUP + i] = top * (1.0 / CODE_MAX)

        @pl.when(step == 0)
        def _():
            pl.semaphore_wait(barrier, peers - 1)

        for i in range(GROUP):
            index = group * GROUP + i

            @pl.when(index != me)
            def _():
                code_copy(index, index, me).start()
                unit_copy(index, index, me).start()

        return carry

    lax.fori_loop(0, groups, forward, 0)

    code_recv[me] = code_send[me]
    unit_recv[me] = unit_send[me]
    member_ref[...] = jnp.transpose(member_wide).astype(jnp.bfloat16)
    gain_rows = jnp.concatenate(
        [jnp.broadcast_to(gains[d], (group_paths, trade_count)) for d in range(local_dates)], axis=0
    )
    gain_cols[...] = jnp.transpose(gain_rows)

    def order_rows(group, carry):
        rows = basis_ref[:, pl.ds(pl.multiple_of(group * group_paths, group_paths), group_paths), :]
        basis_rows[pl.ds(pl.multiple_of(group * group_rows, group_rows), group_rows), :] = (
            rows.reshape(group_rows, basis_count)
        )
        return carry

    lax.fori_loop(0, groups, order_rows, 0)

    def arrived(step, carry):
        source = lax.rem(me + step, peers)
        code_copy(source, source, source).wait_recv()
        unit_copy(source, source, source).wait_recv()
        return carry

    lax.fori_loop(1, peers, arrived, 0)

    def add(trade, totals):
        result = []
        for q in range(date_peers):
            source = trade * date_peers + q
            values = code_recv[source].astype(jnp.int32).astype(jnp.float32)
            result.append(totals[q] + values * unit_recv[source])
        return tuple(result)

    totals = lax.fori_loop(
        0, trade_peers, add,
        tuple(jnp.zeros((chunk_rows, set_count), jnp.float32) for _ in range(date_peers)),
    )
    netted = [
        totals[q][d * own_paths:(d + 1) * own_paths]
        for q in range(date_peers) for d in range(local_dates)
    ]
    date_count = len(netted)
    lags = lag_ref[...]
    direct = []
    for d in range(date_count):
        value = netted[d]
        for lag in range(1, LAG_MAX + 1):
            if d >= lag:
                value = value - jnp.where(lags == lag, netted[d - lag], 0.0)
        direct.append(jnp.maximum(value - limit_ref[...], 0.0) * loss_scale)
    for q in range(date_peers):
        parts = []
        for d in range(q * local_dates, (q + 1) * local_dates):
            value = direct[d]
            for lag in range(1, LAG_MAX + 1):
                if d + lag < date_count:
                    value = value - jnp.where(lags == lag, direct[d + lag], 0.0)
            parts.append(value)
        adj_send[q] = jnp.concatenate(parts, axis=0).astype(jnp.bfloat16)

    def spread_out(step, carry):
        adj_copy(lax.rem(me + peers // 2 + step, peers), me).start()
        return carry

    lax.fori_loop(0, peers // 2, spread_out, 0)

    def spread_near(step, carry):
        adj_copy(lax.rem(me + step, peers), me).start()
        return carry

    lax.fori_loop(1, peers // 2, spread_near, 0)
    adj_recv[me] = adj_send[my_date]

    def backward(step, carry):
        group = lax.rem(my_group + step, groups)
        for i in range(GROUP):
            index = group * GROUP + i

            @pl.when(index != me)
            def _():
                adj_copy(index, index).wait_recv()

        block = adj_recv[pl.ds(pl.multiple_of(group * GROUP, GROUP), GROUP)].astype(jnp.float32)
        block = block.reshape(GROUP, local_dates, own_paths, set_count)
        block = jnp.concatenate(
            [block[i, d] for d in range(local_dates) for i in range(GROUP)], axis=0
        ).astype(jnp.bfloat16)
        spread = lax.dot_general(member_ref[...], block, NT, preferred_element_type=jnp.float32)
        scaled_ref[:, pl.ds(pl.multiple_of(group * group_rows, group_rows), group_rows)] = (
            spread * gain_cols[...]
        ).astype(jnp.bfloat16)
        return carry

    lax.fori_loop(0, groups, backward, 0)

    def half_copy(step):
        q = lax.rem(my_date + step, date_peers)
        return pltpu.make_async_remote_copy(
            src_ref=half_send.at[step - 1], dst_ref=half_recv.at[step - 1],
            send_sem=half_ss.at[step - 1], recv_sem=half_rs.at[step - 1],
            device_id={"dates": q}, device_id_type=pl.DeviceIdType.MESH,
        )

    def columns(q):
        return basis_rows[:, pl.ds(pl.multiple_of(q * half, half), half)]

    for step in range(1, date_peers):
        q = lax.rem(my_date + step, date_peers)
        half_send[step - 1] = jnp.dot(scaled_ref[...], columns(q), preferred_element_type=jnp.float32)
        half_copy(step).start()
    total = jnp.dot(scaled_ref[...], columns(my_date), preferred_element_type=jnp.float32)
    for step in range(1, date_peers):
        half_copy(step).wait_recv()
        total = total + half_recv[step - 1]
    out_ref[...] = total

    def sent(step, carry):
        index = lax.rem(me + step, peers)
        code_copy(index, index, me).wait_send()
        unit_copy(index, index, me).wait_send()
        adj_copy(index, me).wait_send()
        return carry

    lax.fori_loop(1, peers, sent, 0)
    for step in range(1, date_peers):
        half_copy(step).wait_send()


def on_device(
    trade_peers, date_peers,
    basis_values, coefficients, set_map, trade_type, type_gain, set_lags, thresholds,
):
    local_dates, path_count, basis_count = basis_values.shape
    trade_count = coefficients.shape[0]
    set_count = thresholds.shape[0]
    peers = trade_peers * date_peers
    own_paths = path_count // peers
    chunk = local_dates * own_paths
    group_rows = chunk * GROUP
    half = basis_count // date_peers
    loss_scale = 2.0 / math.sqrt(local_dates * date_peers * path_count)
    vmem = pl.BlockSpec(memory_space=pltpu.VMEM)
    dma = pltpu.SemaphoreType.DMA
    return pl.pallas_call(
        functools.partial(kernel, trade_peers, date_peers, loss_scale),
        out_shape=jax.ShapeDtypeStruct((trade_count, half), jnp.float32),
        in_specs=[pl.BlockSpec(memory_space=pltpu.SMEM)] + [vmem] * 6,
        out_specs=vmem,
        scratch_shapes=[
            pltpu.VMEM((peers, chunk, set_count), jnp.int16),
            pltpu.VMEM((peers, chunk, set_count), jnp.int16),
            pltpu.VMEM((peers, 1, set_count), jnp.float32),
            pltpu.VMEM((peers, 1, set_count), jnp.float32),
            pltpu.VMEM((date_peers, chunk, set_count), jnp.bfloat16),
            pltpu.VMEM((peers, chunk, set_count), jnp.bfloat16),
            pltpu.VMEM((trade_count, set_count), jnp.bfloat16),
            pltpu.VMEM((trade_count, group_rows), jnp.float32),
            pltpu.VMEM((path_count * local_dates, basis_count), jnp.bfloat16),
            pltpu.VMEM((trade_count, path_count * local_dates), jnp.bfloat16),
            pltpu.VMEM((date_peers - 1, trade_count, half), jnp.float32),
            pltpu.VMEM((date_peers - 1, trade_count, half), jnp.float32),
            dma((peers,)), dma((peers,)), dma((peers,)), dma((peers,)),
            dma((peers,)), dma((peers,)), dma((date_peers - 1,)), dma((date_peers - 1,)),
        ],
        compiler_params=pltpu.CompilerParams(
            collective_id=0, has_side_effects=True, vmem_limit_bytes=60 * 1024 * 1024
        ),
    )(
        type_gain, basis_values, coefficients, set_map.reshape(1, -1), trade_type.reshape(1, -1),
        set_lags.reshape(1, -1), thresholds.reshape(1, -1),
    )


def solution(mesh):
    return jax.shard_map(
        functools.partial(on_device, mesh.shape["trades"], mesh.shape["dates"]),
        mesh=mesh,
        in_specs=(
            P("dates", "groups", None),
            P("trades", None),
            P("trades"),
            P("trades"),
            P("dates", None),
            P(),
            P(),
        ),
        out_specs=P(("groups", "trades"), "dates"),
        check_vma=False,
    )
```

```python
import functools
import math

import jax
import jax.numpy as jnp
from jax import lax
from jax.experimental import pallas as pl
from jax.experimental.pallas import tpu as pltpu
from jax.sharding import PartitionSpec as P

LAG_MAX = 2
GROUP = 8
CODE_MAX = 32767.0
NT = (((1,), (1,)), ((), ()))


def kernel(
    trade_peers, date_peers, loss_scale,
    gain_in, basis_in, coef_in, set_in, type_in, lag_in, limit_in,
    out_ref,
    gain_ref, basis_ref, coef_ref, set_ref, type_ref, lag_ref, limit_ref, load_sem,
    code_send, code_recv, unit_send, unit_recv, adj_send, adj_recv,
    member_ref, gain_cols, basis_rows, scaled_ref, half_send, half_recv,
    code_ss, code_rs, unit_ss, unit_rs, adj_ss, adj_rs, half_ss, half_rs,
):
    peers = trade_peers * date_peers
    my_trade = lax.axis_index("trades")
    my_date = lax.axis_index("dates")
    me = my_trade * date_peers + my_date
    local_dates, path_count, basis_count = basis_ref.shape
    trade_count = coef_ref.shape[0]
    set_count = limit_ref.shape[1]
    type_count = gain_ref.shape[1]
    own_paths = path_count // peers
    groups = peers // GROUP
    group_paths = GROUP * own_paths
    group_rows = local_dates * group_paths
    chunk_rows = local_dates * own_paths
    half = basis_count // date_peers

    def device(index):
        return {"trades": index // date_peers, "dates": index % date_peers}

    barrier = pltpu.get_barrier_semaphore()

    def greet(step, carry):
        pl.semaphore_signal(
            barrier, inc=1, device_id=device(lax.rem(me + step, peers)),
            device_id_type=pl.DeviceIdType.MESH,
        )
        return carry

    lax.fori_loop(1, peers, greet, 0, unroll=peers <= 16)
    loads = [
        pltpu.make_async_copy(source, target, load_sem.at[i])
        for i, (source, target) in enumerate((
            (type_in, type_ref), (gain_in, gain_ref), (set_in, set_ref), (basis_in, basis_ref),
            (coef_in, coef_ref), (lag_in, lag_ref), (limit_in, limit_ref),
        ))
    ]
    for load in loads:
        load.start()
    for load in loads[:3]:
        load.wait()

    def code_copy(index, slot_here, slot_there):
        return pltpu.make_async_remote_copy(
            src_ref=code_send.at[slot_here], dst_ref=code_recv.at[slot_there],
            send_sem=code_ss.at[slot_here], recv_sem=code_rs.at[slot_there],
            device_id=device(index), device_id_type=pl.DeviceIdType.MESH,
        )

    def unit_copy(index, slot_here, slot_there):
        return pltpu.make_async_remote_copy(
            src_ref=unit_send.at[slot_here], dst_ref=unit_recv.at[slot_there],
            send_sem=unit_ss.at[slot_here], recv_sem=unit_rs.at[slot_there],
            device_id=device(index), device_id_type=pl.DeviceIdType.MESH,
        )

    def adj_copy(index, slot_there):
        return pltpu.make_async_remote_copy(
            src_ref=adj_send.at[index % date_peers], dst_ref=adj_recv.at[slot_there],
            send_sem=adj_ss.at[index], recv_sem=adj_rs.at[slot_there],
            device_id=device(index), device_id_type=pl.DeviceIdType.MESH,
        )

    types = type_ref[...]
    table = gain_ref[...]
    gains = []
    for d in range(local_dates):
        row = jnp.zeros_like(types, dtype=jnp.float32)
        for y in range(type_count):
            row = jnp.where(types == y, table[d:d + 1, y:y + 1], row)
        gains.append(row)
    set_ids = lax.broadcasted_iota(jnp.int32, (set_count, trade_count), 0)
    member_wide = jnp.where(set_ids == set_ref[...], 1.0, 0.0)
    member = member_wide.astype(jnp.bfloat16)

    my_group = me // GROUP
    for load in loads[3:]:
        load.wait()

    def forward(step, carry):
        group = lax.rem(my_group + 1 + step, groups)
        rows = basis_ref[:, pl.ds(pl.multiple_of(group * group_paths, group_paths), group_paths), :]
        raw = lax.dot_general(
            rows.reshape(group_rows, basis_count), coef_ref[...], NT,
            preferred_element_type=jnp.float32,
        )
        prices = jnp.concatenate(
            [raw[d * group_paths:(d + 1) * group_paths] * gains[d] for d in range(local_dates)], axis=0
        ).astype(jnp.bfloat16)
        part = lax.dot_general(prices, member, NT, preferred_element_type=jnp.float32)
        part = part.reshape(local_dates, GROUP, own_paths, set_count)
        for i in range(GROUP):
            chunk = part[:, i].reshape(chunk_rows, set_count)
            top = jnp.maximum(jnp.max(jnp.abs(chunk), axis=0, keepdims=True), 1e-30)
            codes = jnp.round(chunk * (CODE_MAX / top)).astype(jnp.int32)
            code_send[group * GROUP + i] = codes.astype(jnp.int16)
            unit_send[group * GROUP + i] = top * (1.0 / CODE_MAX)

        @pl.when(step == 0)
        def _():
            pl.semaphore_wait(barrier, peers - 1)

        for i in range(GROUP):
            index = group * GROUP + i

            @pl.when(index != me)
            def _():
                code_copy(index, index, me).start()
                unit_copy(index, index, me).start()

        return carry

    lax.fori_loop(0, groups, forward, 0, unroll=groups <= 2)

    code_recv[me] = code_send[me]
    unit_recv[me] = unit_send[me]
    member_ref[...] = jnp.transpose(member_wide).astype(jnp.bfloat16)
    gain_rows = jnp.concatenate(
        [jnp.broadcast_to(gains[d], (group_paths, trade_count)) for d in range(local_dates)], axis=0
    )
    gain_cols[...] = jnp.transpose(gain_rows)

    def order_rows(group, carry):
        rows = basis_ref[:, pl.ds(pl.multiple_of(group * group_paths, group_paths), group_paths), :]
        basis_rows[pl.ds(pl.multiple_of(group * group_rows, group_rows), group_rows), :] = (
            rows.reshape(group_rows, basis_count)
        )
        return carry

    lax.fori_loop(0, groups, order_rows, 0, unroll=groups <= 2)

    def arrived(step, carry):
        source = lax.rem(me + step, peers)
        code_copy(source, source, source).wait_recv()
        unit_copy(source, source, source).wait_recv()
        return carry

    lax.fori_loop(1, peers, arrived, 0, unroll=peers <= 16)

    def add(trade, totals):
        result = []
        for q in range(date_peers):
            source = trade * date_peers + q
            values = code_recv[source].astype(jnp.int32).astype(jnp.float32)
            result.append(totals[q] + values * unit_recv[source])
        return tuple(result)

    totals = lax.fori_loop(
        0, trade_peers, add,
        tuple(jnp.zeros((chunk_rows, set_count), jnp.float32) for _ in range(date_peers)),
        unroll=peers <= 16,
    )
    netted = [
        totals[q][d * own_paths:(d + 1) * own_paths]
        for q in range(date_peers) for d in range(local_dates)
    ]
    date_count = len(netted)
    lags = lag_ref[...]
    direct = []
    for d in range(date_count):
        value = netted[d]
        for lag in range(1, LAG_MAX + 1):
            if d >= lag:
                value = value - jnp.where(lags == lag, netted[d - lag], 0.0)
        direct.append(jnp.maximum(value - limit_ref[...], 0.0) * loss_scale)
    for q in range(date_peers):
        parts = []
        for d in range(q * local_dates, (q + 1) * local_dates):
            value = direct[d]
            for lag in range(1, LAG_MAX + 1):
                if d + lag < date_count:
                    value = value - jnp.where(lags == lag, direct[d + lag], 0.0)
            parts.append(value)
        adj_send[q] = jnp.concatenate(parts, axis=0).astype(jnp.bfloat16)

    def spread_out(step, carry):
        adj_copy(lax.rem(me + step, peers), me).start()
        return carry

    lax.fori_loop(1, peers, spread_out, 0, unroll=peers <= 16)
    adj_recv[me] = adj_send[my_date]

    def backward(step, carry):
        group = lax.rem(my_group + step, groups)
        for i in range(GROUP):
            index = group * GROUP + i

            @pl.when(index != me)
            def _():
                adj_copy(index, index).wait_recv()

        block = adj_recv[pl.ds(pl.multiple_of(group * GROUP, GROUP), GROUP)].astype(jnp.float32)
        block = block.reshape(GROUP, local_dates, own_paths, set_count)
        block = jnp.concatenate(
            [block[i, d] for d in range(local_dates) for i in range(GROUP)], axis=0
        ).astype(jnp.bfloat16)
        spread = lax.dot_general(member_ref[...], block, NT, preferred_element_type=jnp.float32)
        scaled_ref[:, pl.ds(pl.multiple_of(group * group_rows, group_rows), group_rows)] = (
            spread * gain_cols[...]
        ).astype(jnp.bfloat16)
        return carry

    lax.fori_loop(0, groups, backward, 0, unroll=groups <= 2)

    def half_copy(step):
        q = lax.rem(my_date + step, date_peers)
        return pltpu.make_async_remote_copy(
            src_ref=half_send.at[step - 1], dst_ref=half_recv.at[step - 1],
            send_sem=half_ss.at[step - 1], recv_sem=half_rs.at[step - 1],
            device_id={"dates": q}, device_id_type=pl.DeviceIdType.MESH,
        )

    def columns(q):
        return basis_rows[:, pl.ds(pl.multiple_of(q * half, half), half)]

    for step in range(1, date_peers):
        q = lax.rem(my_date + step, date_peers)
        half_send[step - 1] = jnp.dot(scaled_ref[...], columns(q), preferred_element_type=jnp.float32)
        half_copy(step).start()
    total = jnp.dot(scaled_ref[...], columns(my_date), preferred_element_type=jnp.float32)
    def sent(step, carry):
        index = lax.rem(me + step, peers)
        code_copy(index, index, me).wait_send()
        unit_copy(index, index, me).wait_send()
        adj_copy(index, me).wait_send()
        return carry

    lax.fori_loop(1, peers, sent, 0, unroll=peers <= 16)
    for step in range(1, date_peers):
        half_copy(step).wait_recv()
        total = total + half_recv[step - 1]
    out_ref[...] = total

    for step in range(1, date_peers):
        half_copy(step).wait_send()


def on_device(
    trade_peers, date_peers,
    basis_values, coefficients, set_map, trade_type, type_gain, set_lags, thresholds,
):
    local_dates, path_count, basis_count = basis_values.shape
    trade_count = coefficients.shape[0]
    set_count = thresholds.shape[0]
    peers = trade_peers * date_peers
    own_paths = path_count // peers
    chunk = local_dates * own_paths
    group_rows = chunk * GROUP
    half = basis_count // date_peers
    loss_scale = 2.0 / math.sqrt(local_dates * date_peers * path_count)
    vmem_limit = min(60, 20 + 4 * local_dates * path_count // 512) * 1024 * 1024
    vmem = pl.BlockSpec(memory_space=pltpu.VMEM)
    dma = pltpu.SemaphoreType.DMA
    return pl.pallas_call(
        functools.partial(kernel, trade_peers, date_peers, loss_scale),
        out_shape=jax.ShapeDtypeStruct((trade_count, half), jnp.float32),
        in_specs=[pl.BlockSpec(memory_space=pltpu.HBM)] * 7,
        out_specs=vmem,
        scratch_shapes=[
            pltpu.VMEM(type_gain.shape, jnp.float32),
            pltpu.VMEM(basis_values.shape, jnp.bfloat16),
            pltpu.VMEM(coefficients.shape, jnp.bfloat16),
            pltpu.VMEM((1, trade_count), jnp.int32),
            pltpu.VMEM((1, trade_count), jnp.int32),
            pltpu.VMEM((1, set_count), jnp.int32),
            pltpu.VMEM((1, set_count), jnp.float32),
            dma((7,)),
            pltpu.VMEM((peers, chunk, set_count), jnp.int16),
            pltpu.VMEM((peers, chunk, set_count), jnp.int16),
            pltpu.VMEM((peers, 1, set_count), jnp.float32),
            pltpu.VMEM((peers, 1, set_count), jnp.float32),
            pltpu.VMEM((date_peers, chunk, set_count), jnp.bfloat16),
            pltpu.VMEM((peers, chunk, set_count), jnp.bfloat16),
            pltpu.VMEM((trade_count, set_count), jnp.bfloat16),
            pltpu.VMEM((trade_count, group_rows), jnp.float32),
            pltpu.VMEM((path_count * local_dates, basis_count), jnp.bfloat16),
            pltpu.VMEM((trade_count, path_count * local_dates), jnp.bfloat16),
            pltpu.VMEM((date_peers - 1, trade_count, half), jnp.float32),
            pltpu.VMEM((date_peers - 1, trade_count, half), jnp.float32),
            dma((peers,)), dma((peers,)), dma((peers,)), dma((peers,)),
            dma((peers,)), dma((peers,)), dma((date_peers - 1,)), dma((date_peers - 1,)),
        ],
        compiler_params=pltpu.CompilerParams(
            collective_id=0, has_side_effects=True, vmem_limit_bytes=vmem_limit
        ),
    )(
        *[
            pltpu.with_memory_space_constraint(x, pltpu.HBM)
            for x in (
                type_gain, basis_values, coefficients, set_map.reshape(1, -1),
                trade_type.reshape(1, -1), set_lags.reshape(1, -1), thresholds.reshape(1, -1),
            )
        ]
    )


def solution(mesh):
    return jax.shard_map(
        functools.partial(on_device, mesh.shape["trades"], mesh.shape["dates"]),
        mesh=mesh,
        in_specs=(
            P("dates", "groups", None),
            P("trades", None),
            P("trades"),
            P("trades"),
            P("dates", None),
            P(),
            P(),
        ),
        out_specs=P(("groups", "trades"), "dates"),
        check_vma=False,
    )
```

```python
import functools
import math

import jax
import jax.numpy as jnp
from jax import lax
from jax.experimental import pallas as pl
from jax.experimental.pallas import tpu as pltpu
from jax.sharding import PartitionSpec as P

LAG_MAX = 2
GROUP = 8
PIECES = 2
CODE_MAX = 32767.0
NT = (((1,), (1,)), ((), ()))


def kernel(
    trade_peers, date_peers, loss_scale,
    gain_in, basis_in, coef_in, set_in, type_in, lag_in, limit_in,
    out_ref,
    gain_ref, basis_ref, coef_ref, set_ref, type_ref, lag_ref, limit_ref, load_sem,
    code_send, code_recv, unit_send, unit_recv, adj_send, adj_recv,
    member_ref, gain_cols, basis_rows, scaled_ref, half_send, half_recv,
    code_ss, code_rs, unit_ss, unit_rs, adj_ss, adj_rs, half_ss, half_rs,
):
    peers = trade_peers * date_peers
    my_trade = lax.axis_index("trades")
    my_date = lax.axis_index("dates")
    me = my_trade * date_peers + my_date
    local_dates, path_count, basis_count = basis_ref.shape
    trade_count = coef_ref.shape[0]
    set_count = limit_ref.shape[1]
    type_count = gain_ref.shape[1]
    own_paths = path_count // peers
    groups = peers // GROUP
    group_paths = GROUP * own_paths
    group_rows = local_dates * group_paths
    chunk_rows = local_dates * own_paths
    half = basis_count // date_peers

    def device(index):
        return {"trades": index // date_peers, "dates": index % date_peers}

    barrier = pltpu.get_barrier_semaphore()

    def greet(step, carry):
        pl.semaphore_signal(
            barrier, inc=1, device_id=device(lax.rem(me + step, peers)),
            device_id_type=pl.DeviceIdType.MESH,
        )
        return carry

    lax.fori_loop(1, peers, greet, 0, unroll=peers <= 16)
    loads = [
        pltpu.make_async_copy(source, target, load_sem.at[i])
        for i, (source, target) in enumerate((
            (type_in, type_ref), (gain_in, gain_ref), (set_in, set_ref), (basis_in, basis_ref),
            (coef_in, coef_ref), (lag_in, lag_ref), (limit_in, limit_ref),
        ))
    ]
    for load in loads:
        load.start()
    for load in loads[:3]:
        load.wait()

    def code_copy(index, slot_here, slot_there):
        return pltpu.make_async_remote_copy(
            src_ref=code_send.at[slot_here], dst_ref=code_recv.at[slot_there],
            send_sem=code_ss.at[slot_here], recv_sem=code_rs.at[slot_there],
            device_id=device(index), device_id_type=pl.DeviceIdType.MESH,
        )

    def unit_copy(index, slot_here, slot_there):
        return pltpu.make_async_remote_copy(
            src_ref=unit_send.at[slot_here], dst_ref=unit_recv.at[slot_there],
            send_sem=unit_ss.at[slot_here], recv_sem=unit_rs.at[slot_there],
            device_id=device(index), device_id_type=pl.DeviceIdType.MESH,
        )

    def adj_copy(index, slot_there):
        return pltpu.make_async_remote_copy(
            src_ref=adj_send.at[index % date_peers], dst_ref=adj_recv.at[slot_there],
            send_sem=adj_ss.at[index], recv_sem=adj_rs.at[slot_there],
            device_id=device(index), device_id_type=pl.DeviceIdType.MESH,
        )

    types = type_ref[...]
    table = gain_ref[...]
    gains = []
    for d in range(local_dates):
        row = jnp.zeros_like(types, dtype=jnp.float32)
        for y in range(type_count):
            row = jnp.where(types == y, table[d:d + 1, y:y + 1], row)
        gains.append(row)
    set_ids = lax.broadcasted_iota(jnp.int32, (set_count, trade_count), 0)
    member_wide = jnp.where(set_ids == set_ref[...], 1.0, 0.0)
    member = member_wide.astype(jnp.bfloat16)

    my_group = me // GROUP
    for load in loads[3:]:
        load.wait()

    def forward(step, carry):
        group = lax.rem(my_group + 1 + step, groups)
        rows = basis_ref[:, pl.ds(pl.multiple_of(group * group_paths, group_paths), group_paths), :]
        raw = lax.dot_general(
            rows.reshape(group_rows, basis_count), coef_ref[...], NT,
            preferred_element_type=jnp.float32,
        )
        prices = jnp.concatenate(
            [raw[d * group_paths:(d + 1) * group_paths] * gains[d] for d in range(local_dates)], axis=0
        ).astype(jnp.bfloat16)
        part = lax.dot_general(prices, member, NT, preferred_element_type=jnp.float32)
        part = part.reshape(local_dates, GROUP, own_paths, set_count)
        for i in range(GROUP):
            chunk = part[:, i].reshape(chunk_rows, set_count)
            top = jnp.maximum(jnp.max(jnp.abs(chunk), axis=0, keepdims=True), 1e-30)
            codes = jnp.round(chunk * (CODE_MAX / top)).astype(jnp.int32)
            code_send[group * GROUP + i] = codes.astype(jnp.int16)
            unit_send[group * GROUP + i] = top * (1.0 / CODE_MAX)

        return carry

    lax.fori_loop(0, groups, forward, 0, unroll=groups <= 2)
    pl.semaphore_wait(barrier, peers - 1)

    def deal(step, carry):
        index = lax.rem(me + step, peers)
        code_copy(index, index, me).start()
        unit_copy(index, index, me).start()
        return carry

    lax.fori_loop(1, peers, deal, 0, unroll=peers <= 16)

    code_recv[me] = code_send[me]
    unit_recv[me] = unit_send[me]
    member_ref[...] = jnp.transpose(member_wide).astype(jnp.bfloat16)
    gain_rows = jnp.concatenate(
        [jnp.broadcast_to(gains[d], (group_paths, trade_count)) for d in range(local_dates)], axis=0
    )
    gain_cols[...] = jnp.transpose(gain_rows)

    def order_rows(group, carry):
        rows = basis_ref[:, pl.ds(pl.multiple_of(group * group_paths, group_paths), group_paths), :]
        basis_rows[pl.ds(pl.multiple_of(group * group_rows, group_rows), group_rows), :] = (
            rows.reshape(group_rows, basis_count)
        )
        return carry

    lax.fori_loop(0, groups, order_rows, 0, unroll=groups <= 2)

    def arrived(step, carry):
        source = lax.rem(me + step, peers)
        code_copy(source, source, source).wait_recv()
        unit_copy(source, source, source).wait_recv()
        return carry

    lax.fori_loop(1, peers, arrived, 0, unroll=peers <= 16)

    def add(trade, totals):
        result = []
        for q in range(date_peers):
            source = trade * date_peers + q
            values = code_recv[source].astype(jnp.int32).astype(jnp.float32)
            result.append(totals[q] + values * unit_recv[source])
        return tuple(result)

    totals = lax.fori_loop(
        0, trade_peers, add,
        tuple(jnp.zeros((chunk_rows, set_count), jnp.float32) for _ in range(date_peers)),
        unroll=peers <= 16,
    )
    netted = [
        totals[q][d * own_paths:(d + 1) * own_paths]
        for q in range(date_peers) for d in range(local_dates)
    ]
    date_count = len(netted)
    lags = lag_ref[...]
    direct = []
    for d in range(date_count):
        value = netted[d]
        for lag in range(1, LAG_MAX + 1):
            if d >= lag:
                value = value - jnp.where(lags == lag, netted[d - lag], 0.0)
        direct.append(jnp.maximum(value - limit_ref[...], 0.0) * loss_scale)
    for q in range(date_peers):
        parts = []
        for d in range(q * local_dates, (q + 1) * local_dates):
            value = direct[d]
            for lag in range(1, LAG_MAX + 1):
                if d + lag < date_count:
                    value = value - jnp.where(lags == lag, direct[d + lag], 0.0)
            parts.append(value)
        adj_send[q] = jnp.concatenate(parts, axis=0).astype(jnp.bfloat16)

    def spread_out(step, carry):
        adj_copy(lax.rem(me + step, peers), me).start()
        return carry

    lax.fori_loop(1, peers, spread_out, 0, unroll=peers <= 16)
    adj_recv[me] = adj_send[my_date]

    def backward(step, carry):
        group = lax.rem(my_group + step, groups)
        for i in range(GROUP):
            index = group * GROUP + i

            @pl.when(index != me)
            def _():
                adj_copy(index, index).wait_recv()

        block = adj_recv[pl.ds(pl.multiple_of(group * GROUP, GROUP), GROUP)].astype(jnp.float32)
        block = block.reshape(GROUP, local_dates, own_paths, set_count)
        block = jnp.concatenate(
            [block[i, d] for d in range(local_dates) for i in range(GROUP)], axis=0
        ).astype(jnp.bfloat16)
        spread = lax.dot_general(member_ref[...], block, NT, preferred_element_type=jnp.float32)
        scaled_ref[:, pl.ds(pl.multiple_of(group * group_rows, group_rows), group_rows)] = (
            spread * gain_cols[...]
        ).astype(jnp.bfloat16)
        return carry

    lax.fori_loop(0, groups, backward, 0, unroll=groups <= 2)

    piece_rows = trade_count // PIECES

    def half_copy(step, piece):
        rows = pl.ds(piece * piece_rows, piece_rows)
        q = lax.rem(my_date + step, date_peers)
        return pltpu.make_async_remote_copy(
            src_ref=half_send.at[step - 1, rows], dst_ref=half_recv.at[step - 1, rows],
            send_sem=half_ss.at[step - 1, piece], recv_sem=half_rs.at[step - 1, piece],
            device_id={"dates": q}, device_id_type=pl.DeviceIdType.MESH,
        )

    def columns(q):
        return basis_rows[:, pl.ds(pl.multiple_of(q * half, half), half)]

    for step in range(1, date_peers):
        q = lax.rem(my_date + step, date_peers)
        for piece in range(PIECES):
            rows = pl.ds(piece * piece_rows, piece_rows)
            half_send[step - 1, rows] = jnp.dot(
                scaled_ref[rows], columns(q), preferred_element_type=jnp.float32
            )
            half_copy(step, piece).start()
    out_ref[...] = jnp.dot(scaled_ref[...], columns(my_date), preferred_element_type=jnp.float32)

    def sent(step, carry):
        index = lax.rem(me + step, peers)
        code_copy(index, index, me).wait_send()
        unit_copy(index, index, me).wait_send()
        adj_copy(index, me).wait_send()
        return carry

    lax.fori_loop(1, peers, sent, 0, unroll=peers <= 16)
    for step in range(1, date_peers):
        for piece in range(PIECES):
            rows = pl.ds(piece * piece_rows, piece_rows)
            half_copy(step, piece).wait_recv()
            out_ref[rows] += half_recv[step - 1, rows]

    for step in range(1, date_peers):
        for piece in range(PIECES):
            half_copy(step, piece).wait_send()


def on_device(
    trade_peers, date_peers,
    basis_values, coefficients, set_map, trade_type, type_gain, set_lags, thresholds,
):
    local_dates, path_count, basis_count = basis_values.shape
    trade_count = coefficients.shape[0]
    set_count = thresholds.shape[0]
    peers = trade_peers * date_peers
    own_paths = path_count // peers
    chunk = local_dates * own_paths
    group_rows = chunk * GROUP
    half = basis_count // date_peers
    loss_scale = 2.0 / math.sqrt(local_dates * date_peers * path_count)
    vmem_limit = min(60, 20 + 4 * local_dates * path_count // 512) * 1024 * 1024
    vmem = pl.BlockSpec(memory_space=pltpu.VMEM)
    dma = pltpu.SemaphoreType.DMA
    return pl.pallas_call(
        functools.partial(kernel, trade_peers, date_peers, loss_scale),
        out_shape=jax.ShapeDtypeStruct((trade_count, half), jnp.float32),
        in_specs=[pl.BlockSpec(memory_space=pltpu.HBM)] * 7,
        out_specs=vmem,
        scratch_shapes=[
            pltpu.VMEM(type_gain.shape, jnp.float32),
            pltpu.VMEM(basis_values.shape, jnp.bfloat16),
            pltpu.VMEM(coefficients.shape, jnp.bfloat16),
            pltpu.VMEM((1, trade_count), jnp.int32),
            pltpu.VMEM((1, trade_count), jnp.int32),
            pltpu.VMEM((1, set_count), jnp.int32),
            pltpu.VMEM((1, set_count), jnp.float32),
            dma((7,)),
            pltpu.VMEM((peers, chunk, set_count), jnp.int16),
            pltpu.VMEM((peers, chunk, set_count), jnp.int16),
            pltpu.VMEM((peers, 1, set_count), jnp.float32),
            pltpu.VMEM((peers, 1, set_count), jnp.float32),
            pltpu.VMEM((date_peers, chunk, set_count), jnp.bfloat16),
            pltpu.VMEM((peers, chunk, set_count), jnp.bfloat16),
            pltpu.VMEM((trade_count, set_count), jnp.bfloat16),
            pltpu.VMEM((trade_count, group_rows), jnp.float32),
            pltpu.VMEM((path_count * local_dates, basis_count), jnp.bfloat16),
            pltpu.VMEM((trade_count, path_count * local_dates), jnp.bfloat16),
            pltpu.VMEM((date_peers - 1, trade_count, half), jnp.float32),
            pltpu.VMEM((date_peers - 1, trade_count, half), jnp.float32),
            dma((peers,)), dma((peers,)), dma((peers,)), dma((peers,)),
            dma((peers,)), dma((peers,)), dma((date_peers - 1, PIECES)), dma((date_peers - 1, PIECES)),
        ],
        compiler_params=pltpu.CompilerParams(
            collective_id=0, has_side_effects=True, vmem_limit_bytes=vmem_limit
        ),
    )(
        *[
            pltpu.with_memory_space_constraint(x, pltpu.HBM)
            for x in (
                type_gain, basis_values, coefficients, set_map.reshape(1, -1),
                trade_type.reshape(1, -1), set_lags.reshape(1, -1), thresholds.reshape(1, -1),
            )
        ]
    )


def solution(mesh):
    return jax.shard_map(
        functools.partial(on_device, mesh.shape["trades"], mesh.shape["dates"]),
        mesh=mesh,
        in_specs=(
            P("dates", "groups", None),
            P("trades", None),
            P("trades"),
            P("trades"),
            P("dates", None),
            P(),
            P(),
        ),
        out_specs=P(("groups", "trades"), "dates"),
        check_vma=False,
    )
```
